32 devices in a mesh: tiles: 2 (over x), morton: 16 (over z, y, core).
Axes of the slice: x: 2, y: 2, z: 4, core: 2. Of those that a mesh axis runs over, the one named last changes fastest.
Arguments:
- features: bfloat16 [256, 512, 64], P(('tiles', 'morton')), parts along dimension 0, may hold values from -6 to 6
- neighbours: int32 [256, 27], P(('tiles', 'morton')), parts along dimension 0, may hold values from -1 to 127, as said below
- occupancy: int32 [256, 16], P(('tiles', 'morton')), parts along dimension 0, may hold values from -2147483648 to 2147483647, as said below
- conv_one: bfloat16 [27, 64, 64], replicated, may hold values from -0.21875 to 0.21875
- first_reduce_kernel: bfloat16 [8, 64, 128], replicated, may hold values from -0.5 to 0.5
- conv_two: bfloat16 [27, 128, 128], replicated, may hold values from -0.1875 to 0.1875
- second_reduce_kernel: bfloat16 [8, 128, 256], replicated, may hold values from -0.375 to 0.375
- conv_three: bfloat16 [27, 256, 256], replicated, may hold values from -0.125 to 0.125
Outputs:
- first_level_features: bfloat16 [256, 512, 64], P(('tiles', 'morton')), parts along dimension 0
- second_level_features: bfloat16 [256, 64, 128], P(('tiles', 'morton')), parts along dimension 0
- skip_three: bfloat16 [256, 8, 256], P(('tiles', 'morton')), parts along dimension 0
The draws below stay inside these ranges and needn't reach their ends.
There are 2 independent parts, one for each index of `tiles`. The reference program is written for one: setup_inputs(seed, part) draws one part's arguments, and reference() takes and returns one part's arrays. A program takes and returns all parts, laid end to end along the dimension named above; an argument that names none is the same for every part. Nothing has to cross between parts.
Inputs may be any that keep to these rules, and one draw needn't show every extreme that they name: `neighbours`: bricks are numbered by x slice, then by cell of the slice's 4 x 4 cross-section in rising order, 8 occupied bricks to a slice. Entry 9 (a+1) + 3 (c+1) + (e+1) of a brick's row is the number of the brick at offset (a, c, e), or -1 if that cell is empty or outside the tile; entry 13 is the brick itself. Every neighbour lies in the brick's own slice or in an adjacent one. Bit k, the lowest being bit 0, of word w of a brick's row is the occupancy of voxel 32 w + k; bit 31 is the sign bit of the word.
All inputs are finite; a program needn't handle non-finite values.
Results may differ from the reference program's by a relative error of at most 0.008.
Values may be sent and summed in bfloat16 or wider, within the bound.
A program may use at most 128 MiB of HBM per device.

```python
import jax
import jax.numpy as jnp
from jax import lax

C1 = 64
C2 = 128
C3 = 256
BRICK_EDGE_VOXELS = 8
SLICE_BRICKS = 8
SLICES = 1
BRICKS = 128
V1 = 512
N_MORTON = 16


def draw_neighbours(key, part):
    slice_total = SLICES * N_MORTON
    scores = jax.random.randint(key, (slice_total, 16), 0, 1 << 20, dtype=jnp.int32) * 16 + jnp.arange(16, dtype=jnp.int32)
    order = jnp.argsort(scores, axis=1)
    ranks = jnp.argsort(order, axis=1)
    filled = (ranks < SLICE_BRICKS).astype(jnp.int32)
    rank_cell = (jnp.cumsum(filled, axis=1) - 1).astype(jnp.int32)
    cells = jnp.argsort(1 - filled, axis=1, stable=True)[:, :SLICE_BRICKS].astype(jnp.int32)
    slice_of = jnp.broadcast_to(jnp.arange(slice_total, dtype=jnp.int32)[:, None], cells.shape)
    row_pos = cells // 4
    col_pos = cells % 4
    entries = []
    for first in (-1, 0, 1):
        for second in (-1, 0, 1):
            for third in (-1, 0, 1):
                near_slice = slice_of + first
                near_row = row_pos + second
                near_col = col_pos + third
                inside = (near_slice >= 0) & (near_slice < slice_total) & (near_row >= 0) & (near_row < 4) & (near_col >= 0) & (near_col < 4)
                safe_slice = jnp.clip(near_slice, 0, slice_total - 1)
                safe_cell = jnp.clip(near_row, 0, 3) * 4 + jnp.clip(near_col, 0, 3)
                present = filled[safe_slice, safe_cell] == 1
                number = safe_slice * SLICE_BRICKS + rank_cell[safe_slice, safe_cell]
                entries.append(jnp.where(inside & present, number, -1).astype(jnp.int32))
    return jnp.stack(entries, axis=-1).reshape(slice_total * SLICE_BRICKS, 27)


def draw_occupancy(key, part):
    brick_side = BRICK_EDGE_VOXELS
    key_list = jax.random.split(key, 6)
    voxel_ids = jnp.arange(brick_side ** 3, dtype=jnp.int32)[None, :]
    depth_index = voxel_ids // (brick_side * brick_side)
    row_index = voxel_ids // brick_side % brick_side
    col_index = voxel_ids % brick_side
    facing = jax.random.randint(key_list[0], (BRICKS, 1), 0, 3, dtype=jnp.int32)
    height_base = jax.random.randint(key_list[1], (BRICKS, 1), 0, brick_side, dtype=jnp.int32)
    tilt_pair = jax.random.randint(key_list[2], (BRICKS, 2), -1, 2, dtype=jnp.int32)
    thickness = jax.random.randint(key_list[3], (BRICKS, 1), brick_side // 4, brick_side // 2 + 2, dtype=jnp.int32)
    present = jax.random.randint(key_list[4], (BRICKS, 1), 0, 8, dtype=jnp.int32) > 0
    retained = jax.random.randint(key_list[5], (BRICKS, brick_side ** 3), 0, 8, dtype=jnp.int32) > 0
    across = jnp.where(facing == 0, depth_index, jnp.where(facing == 1, row_index, col_index))
    along_one = jnp.where(facing == 0, row_index, depth_index)
    along_two = jnp.where(facing == 2, row_index, col_index)
    height = height_base - brick_side // 4 + (tilt_pair[:, 0:1] * along_one + tilt_pair[:, 1:2] * along_two) // 2
    offset = across - height
    occupied = (offset >= 0) & (offset < thickness) & retained & present
    bits = occupied.astype(jnp.int32).reshape(BRICKS, brick_side ** 3 // 32, 32)
    shifted = jnp.left_shift(bits, jnp.arange(32, dtype=jnp.int32))
    return jnp.sum(shifted, axis=-1, dtype=jnp.int32).astype(jnp.int32)


def block_levels(own_key, dims, pieces, least, largest):
    def one(axis_at, blocks):
        heights = jax.random.uniform(jax.random.fold_in(jax.random.fold_in(own_key, 6), axis_at), (blocks,), jnp.float32, least / len(pieces), largest / len(pieces))
        return jnp.repeat(jnp.exp(heights), dims[axis_at] // blocks).reshape((-1,) + (1,) * (len(dims) - axis_at - 1))

    factor_of = one(*pieces[0])
    for cut in pieces[1:]:
        factor_of = factor_of * one(*cut)
    return factor_of


def bell_draw(key, extent, width, bound, pieces=(), held_as=jnp.bfloat16):
    array = width * jax.random.normal(key, extent, jnp.float32)
    if pieces:
        array = array * block_levels(key, extent, pieces, -0.22, 0.18)
    return jnp.clip(array, -bound, bound).astype(held_as)


def setup_inputs(seed: int = 0, part: int = 0) -> dict:
    streams_of = jax.random.split(jax.random.key(seed), 9)
    part_splits = jax.random.split(jax.random.fold_in(streams_of[8], part), 9)
    features = bell_draw(part_splits[0], (BRICKS, V1, C1), 1.0, 6.0, ((0, 16),))
    neighbours = draw_neighbours(jax.random.fold_in(jax.random.fold_in(streams_of[8], part), 71), part)
    occupancy = draw_occupancy(jax.random.fold_in(jax.random.fold_in(streams_of[8], part), 71), part)
    conv_one = bell_draw(streams_of[3], (27, C1, C1), (27 * C1 // 2) ** -0.5, 0.21875)
    first_reduce_kernel = bell_draw(streams_of[4], (8, C1, C2), (2 * C1) ** -0.5, 0.5)
    conv_two = bell_draw(streams_of[5], (27, C2, C2), (9 * C2) ** -0.5, 0.1875)
    second_reduce_kernel = bell_draw(streams_of[6], (8, C2, C3), (2 * C2) ** -0.5, 0.375)
    conv_three = bell_draw(streams_of[7], (27, C3, C3), (9 * C3) ** -0.5, 0.125)
    return {"features": features, "neighbours": neighbours, "occupancy": occupancy, "conv_one": conv_one, "first_reduce_kernel": first_reduce_kernel, "conv_two": conv_two, "second_reduce_kernel": second_reduce_kernel, "conv_three": conv_three}


def unpack_bits(packed, voxel_count):
    shifts = jnp.arange(32, dtype=jnp.int32)
    bits = jnp.bitwise_and(jnp.right_shift(packed[:, :, None], shifts), 1)
    return bits.reshape(packed.shape[0], voxel_count).astype(jnp.float32)


def pool_mask(occupied_voxel_mask, brick_extent):
    count = occupied_voxel_mask.shape[0]
    half = brick_extent // 2
    blocks = occupied_voxel_mask.reshape(count, half, 2, half, 2, half, 2)
    blocks = blocks.transpose(0, 1, 3, 5, 2, 4, 6).reshape(count, half * half * half, 8)
    return jnp.max(blocks, axis=-1)


def reduce_resolution(feature_volume, kernel_weight, occupied_voxel_mask, brick_extent):
    count, voxels, chans = feature_volume.shape
    half = brick_extent // 2
    stacked = feature_volume.reshape(count, half, 2, half, 2, half, 2, chans)
    stacked = stacked.transpose(0, 1, 3, 5, 2, 4, 6, 7).reshape(count * voxels // 8, 8 * chans)
    summed = jnp.dot(stacked, kernel_weight.reshape(8 * chans, kernel_weight.shape[2]), preferred_element_type=jnp.float32)
    result = jnp.maximum(summed, 0.0) * occupied_voxel_mask.reshape(-1, 1)
    return result.astype(jnp.bfloat16).reshape(count, voxels // 8, kernel_weight.shape[2])


def pad_bricks(gathered, brick_extent):
    count, chans = gathered.shape[0], gathered.shape[-1]
    table = ((brick_extent - 1, 1, 0), (0, brick_extent, 1), (0, 1, brick_extent + 1))
    padded = jnp.zeros((count, brick_extent + 2, brick_extent + 2, brick_extent + 2, chans), gathered.dtype)
    for first in range(3):
        for second in range(3):
            for third in range(3):
                tap = first * 9 + second * 3 + third
                src_a, len_a, dst_a = table[first]
                src_b, len_b, dst_b = table[second]
                src_c, len_c, dst_c = table[third]
                piece = gathered[:, tap, src_a:src_a + len_a, src_b:src_b + len_b, src_c:src_c + len_c, :]
                padded = padded.at[:, dst_a:dst_a + len_a, dst_b:dst_b + len_b, dst_c:dst_c + len_c, :].set(piece)
    return padded


def convolve_block(extended, sources, occupied_voxel_mask, kernel_weight, brick_extent):
    count = sources.shape[0]
    chans = extended.shape[-1]
    gathered = extended[sources].reshape(count, 27, brick_extent, brick_extent, brick_extent, chans)
    padded = pad_bricks(gathered, brick_extent)
    windows = []
    for first in range(3):
        for second in range(3):
            for third in range(3):
                windows.append(padded[:, first:first + brick_extent, second:second + brick_extent, third:third + brick_extent, :])
    columns = jnp.concatenate(windows, axis=-1).reshape(count * brick_extent ** 3, 27 * chans)
    summed = jnp.dot(columns, kernel_weight.reshape(27 * chans, kernel_weight.shape[2]), preferred_element_type=jnp.float32)
    result = jnp.maximum(summed, 0.0) * occupied_voxel_mask.reshape(-1, 1)
    return result.astype(jnp.bfloat16).reshape(count, brick_extent ** 3, kernel_weight.shape[2])


def run_level(feature_volume, neighbours, occupied_voxel_mask, kernel_weight, brick_extent):
    total, voxels, chans = feature_volume.shape
    extended = jnp.concatenate([feature_volume, jnp.zeros((1, voxels, chans), feature_volume.dtype)], axis=0)
    sources = jnp.where(neighbours < 0, total, neighbours).astype(jnp.int32)
    groups = total // SLICE_BRICKS

    def one_block(pair):
        return convolve_block(extended, pair[0], pair[1], kernel_weight, brick_extent)

    blocks = (sources.reshape(groups, SLICE_BRICKS, 27), occupied_voxel_mask.reshape(groups, SLICE_BRICKS, voxels))
    return lax.map(one_block, blocks).reshape(total, voxels, kernel_weight.shape[2])


def reference(features, neighbours, occupancy, conv_one, first_reduce_kernel, conv_two, second_reduce_kernel, conv_three):
    mask_one = unpack_bits(occupancy, BRICK_EDGE_VOXELS ** 3)
    second_level_mask = pool_mask(mask_one, BRICK_EDGE_VOXELS)
    third_level_mask = pool_mask(second_level_mask, BRICK_EDGE_VOXELS // 2)
    input_one = (features.astype(jnp.float32) * mask_one[:, :, None]).astype(jnp.bfloat16)
    first_level_features = run_level(input_one, neighbours, mask_one, conv_one, BRICK_EDGE_VOXELS)
    second_level_input = reduce_resolution(first_level_features, first_reduce_kernel, second_level_mask, BRICK_EDGE_VOXELS)
    second_level_features = run_level(second_level_input, neighbours, second_level_mask, conv_two, BRICK_EDGE_VOXELS // 2)
    third_level_input = reduce_resolution(second_level_features, second_reduce_kernel, third_level_mask, BRICK_EDGE_VOXELS // 2)
    skip_three = run_level(third_level_input, neighbours, third_level_mask, conv_three, BRICK_EDGE_VOXELS // 4)
    return first_level_features, second_level_features, skip_three
```

```python
import jax
import jax.numpy as jnp
from jax import lax
from jax.experimental import pallas as pl
from jax.experimental.pallas import tpu as pltpu
from jax.sharding import PartitionSpec as P

BRICKS = 8
LANES = 512
F32 = jnp.float32
BF16 = jnp.bfloat16


def iota(shape, dim):
    return lax.broadcasted_iota(jnp.int32, shape, dim)


def band_pairs(source, band):
    @pl.loop(0, 9)
    def _(tap):
        minus, same, plus = (source[3 * tap + e] for e in range(3))
        zero = jnp.zeros_like(same)
        low = jnp.concatenate([same, minus], axis=1)
        high = jnp.concatenate([plus, same], axis=1)
        before = jnp.concatenate([minus, zero], axis=1)
        after = jnp.concatenate([zero, plus], axis=1)
        blank = jnp.zeros((64, 128), BF16)
        rows = (
            (blank, blank), (before, blank),
            (low, blank), (high, before),
            (after, low), (blank, high),
            (blank, after), (blank, blank),
        )
        for at, (left, right) in enumerate(rows):
            band[tap, at * 64 : at * 64 + 64, 0:128] = left
            band[tap, at * 64 : at * 64 + 64, 128:256] = right


def band_single(source, band):
    @pl.loop(0, 9)
    def _(tap):
        minus, same, plus = (source[3 * tap + e] for e in range(3))
        blank = jnp.zeros_like(same)
        rows = ((minus, blank), (same, minus), (plus, same), (blank, plus))
        for at, (left, right) in enumerate(rows):
            band[tap, at * 128 : at * 128 + 128, 0:128] = left
            band[tap, at * 128 : at * 128 + 128, 128:256] = right


def assemble(side, halo, nb, own, low, high, cols):
    row = iota((8, LANES + 2 * halo), 0)

    def source(brick, tap):
        number = nb[brick, tap]
        return jnp.where(number < 0, BRICKS, lax.rem(number, BRICKS))

    @pl.loop(0, BRICKS // 2)
    def _(pair):
        for dx, ref in ((0, low), (1, own), (2, high)):
            index = [
                [[source(2 * pair + b, 9 * dx + 3 * dy + dz) for dz in range(3)] for dy in range(3)]
                for b in range(2)
            ]
            for plane in range(side if dx == 1 else 1):
                at = slice(8 * plane, 8 * plane + 8)
                shifted = [[], [], []]
                for b in range(2):
                    views = []
                    for dy in range(3):
                        before, here, after = index[b][dy]
                        views.append(
                            jnp.concatenate(
                                [
                                    ref[before, at, LANES - halo : LANES],
                                    ref[here, at, :],
                                    ref[after, at, 0:halo],
                                ],
                                axis=1,
                            )
                        )
                    back, mid, front = views
                    shifted[0].append(
                        jnp.where(
                            row == 0,
                            pltpu.roll(back, (9 - side) % 8, 0),
                            pltpu.roll(mid, 1, 0),
                        )
                    )
                    shifted[1].append(mid)
                    shifted[2].append(
                        jnp.where(
                            row == side - 1,
                            pltpu.roll(front, side - 1, 0),
                            pltpu.roll(mid, 7, 0),
                        )
                    )
                to = plane + 1 if dx == 1 else (0 if dx == 0 else side + 1)
                rows = pl.ds(pl.multiple_of(16 * pair, 16), 16)
                for c in range(3):
                    cols[c, to, rows, :] = jnp.concatenate(shifted[c], axis=0).astype(BF16)


def convolve(side, depth, cols, weights, finish):
    chunk = min(side, 4)
    matrix = jnp.concatenate([weights(tap) for tap in range(9)], axis=0)
    for half in range(2):
        lanes = slice(256 * half, 256 * half + depth)
        for first in range(0, side, chunk):
            left = jnp.concatenate(
                [
                    cols[c, first + a : first + a + chunk, :, lanes].reshape(chunk * 64, depth)
                    for a in range(3)
                    for c in range(3)
                ],
                axis=1,
            )
            sums = jnp.dot(left, matrix, preferred_element_type=F32)
            finish(half, first, sums.reshape(chunk, BRICKS, 8, 256))


def rounded(value):
    return value.astype(BF16).astype(F32)


def pool_bits(bits, fine_side, temp, pooled):
    half = fine_side // 2
    count = BRICKS * half * 8
    joined = bits[0 : BRICKS * fine_side * 8, :].reshape(BRICKS * half, 2, 8, 128)
    temp[0:count, :] = (joined[:, 0] | joined[:, 1]).reshape(count, 128)
    temp[count : count + 16, :] = jnp.zeros((16, 128), jnp.int32)
    for at in range(BRICKS * half):
        even = temp[pl.ds(8 * at, 8, stride=2), :]
        odd = temp[pl.ds(8 * at + 1, 8, stride=2), :]
        pooled[8 * at : 8 * at + 8, :] = even | odd


def reduce_level(side, block, fine, kernel, bits, bit_width, emit):
    half = side // 2
    width = 2 * block
    for at in range(LANES // width):
        parts = []
        for ci in range(2):
            for cj in range(2):
                pieces = []
                for lane in range(at * width, (at + 1) * width, 128):
                    pieces.append(
                        jnp.concatenate(
                            [
                                fine[lane // 128, pl.ds((b * side + 2 * i + ci) * 8 + cj, 8, stride=2), :]
                                for b in range(BRICKS)
                                for i in range(half)
                            ],
                            axis=0,
                        )
                    )
                parts += pieces
        left = jnp.concatenate(parts, axis=1).astype(BF16)
        sums = jnp.dot(left, kernel, preferred_element_type=F32)
        mask = ((bits[0 : BRICKS * half * 8, :] >> (bit_width * at)) & ((1 << bit_width) - 1)) != 0
        wide = sums.shape[1]
        for lane in range(0, wide, 128):
            emit(
                at * wide + lane,
                jnp.where(mask, jnp.maximum(sums[:, lane : lane + 128], 0.0), 0.0),
            )


def level_one(nb, feat, occ, low_in, high_in, weights, kernel,
              out, next_own, next_low, next_high, next_bits,
              own, low, high, cols, band, fine, temp, wide, bits, bits_temp):
    band_pairs(weights, band)
    lane = iota((64, 128), 1)
    row = iota((64, 16), 0)
    column = iota((64, 16), 1)
    upper = (lane >= 64).astype(jnp.int32)
    own[BRICKS] = jnp.zeros((64, LANES), F32)
    low[BRICKS] = jnp.zeros((8, LANES), F32)
    high[BRICKS] = jnp.zeros((8, LANES), F32)

    @pl.loop(0, BRICKS)
    def _(b):
        words = jnp.broadcast_to(occ[pl.ds(b, 1), :], (64, 16))
        octet = (words >> (8 * (row % 4))) & 255
        picked = jnp.where(column == row // 4, octet.astype(F32), 0.0)
        mask = jnp.broadcast_to(jnp.sum(picked, axis=1, keepdims=True), (64, 128)).astype(jnp.int32)
        bits[pl.ds(pl.multiple_of(64 * b, 64), 64), :] = mask
        temp[:, 0:64] = feat[b].astype(F32)
        for q in range(4):
            even = temp[pl.ds(2 * q, 64, stride=8), :]
            odd = temp[pl.ds(2 * q + 1, 64, stride=8), :]
            both = jnp.where(lane < 64, even, pltpu.roll(odd, 64, 1))
            own[b, :, 128 * q : 128 * q + 128] = jnp.where(
                ((mask >> (2 * q + upper)) & 1) != 0, both, 0.0
            )
    for ref, source in ((low, low_in), (high, high_in)):
        temp[:, 0:64] = source[...].astype(F32).reshape(512, 64)
        for q in range(4):
            even = temp[pl.ds(2 * q, 64, stride=8), :]
            odd = temp[pl.ds(2 * q + 1, 64, stride=8), :]
            both = jnp.where(lane < 64, even, pltpu.roll(odd, 64, 1))
            ref[0:BRICKS, :, 128 * q : 128 * q + 128] = both.reshape(BRICKS, 8, 128)

    assemble(8, 128, nb, own, low, high, cols)
    small = iota((8, 128), 1)
    small_upper = (small >= 64).astype(jnp.int32)

    def finish(half, first, sums):
        for p in range(sums.shape[0]):
            for b in range(BRICKS):
                at = b * 64 + (first + p) * 8
                mask = bits[at : at + 8, :]
                for part in range(2):
                    q = 2 * half + part
                    fine[q, at : at + 8, :] = rounded(
                        jnp.where(
                            ((mask >> (2 * q + small_upper)) & 1) != 0,
                            jnp.maximum(sums[p, b, :, 128 * part : 128 * part + 128], 0.0),
                            0.0,
                        )
                    )

    convolve(8, 512, cols, lambda tap: band[tap], finish)
    fine[:, 512:528, :] = jnp.zeros((4, 16, 128), F32)
    pool_bits(bits, 8, bits_temp, next_bits)

    def emit(lane_at, value):
        value = value.reshape(BRICKS, 32, 128)
        lanes = slice(lane_at, lane_at + 128)
        next_own[:, :, lanes] = value
        next_low[:, :, lanes] = value[:, 0:8].astype(BF16)
        next_high[:, :, lanes] = value[:, 24:32].astype(BF16)

    reduce_level(8, 64, fine, kernel[...], next_bits, 2, emit)

    @pl.loop(0, BRICKS)
    def _(b):
        for q in range(4):
            both = fine[q, pl.ds(pl.multiple_of(64 * b, 64), 64), :]
            wide[pl.ds(2 * q, 64, stride=8), :] = both
            wide[pl.ds(2 * q + 1, 64, stride=8), :] = pltpu.roll(both, 64, 1)
        out[b] = wide[:, 0:64].astype(BF16)


def fill(own, low, high, own_in, low_in, high_in):
    own[0:BRICKS] = rounded(own_in[...])
    low[0:BRICKS] = low_in[...].astype(F32)
    high[0:BRICKS] = high_in[...].astype(F32)
    for ref in (own, low, high):
        ref[BRICKS] = jnp.zeros(ref.shape[1:], F32)


def level_two(nb, own_in, low_in, high_in, bits, weights, kernel,
              out, next_own, next_low, next_high, next_bits,
              own, low, high, cols, band, fine, wide, bits_temp):
    band_single(weights, band)
    fill(own, low, high, own_in, low_in, high_in)
    assemble(4, 128, nb, own, low, high, cols)

    def finish(half, first, sums):
        for p in range(sums.shape[0]):
            for b in range(BRICKS):
                at = b * 32 + (first + p) * 8
                mask = bits[at : at + 8, :]
                for part in range(2):
                    q = 2 * half + part
                    fine[q, at : at + 8, :] = rounded(
                        jnp.where(
                            ((mask >> (2 * q)) & 3) != 0,
                            jnp.maximum(sums[p, b, :, 128 * part : 128 * part + 128], 0.0),
                            0.0,
                        )
                    )

    convolve(4, 512, cols, lambda tap: band[tap], finish)
    fine[:, 256:272, :] = jnp.zeros((4, 16, 128), F32)
    pool_bits(bits, 4, bits_temp, next_bits)

    def emit(lane_at, value):
        value = value.reshape(BRICKS, 16, 128)
        lanes = slice(lane_at, lane_at + 128)
        next_own[:, :, lanes] = value
        next_low[:, :, lanes] = value[:, 0:8].astype(BF16)
        next_high[:, :, lanes] = value[:, 8:16].astype(BF16)

    reduce_level(4, 128, fine, kernel[...], next_bits, 4, emit)
    for b in range(BRICKS):
        for i in range(4):
            for k in range(4):
                at = b * 32 + 8 * i
                wide[pl.ds(64 * b + 16 * i + k, 4, stride=4), :] = fine[k, at : at + 4, :]
    out[...] = wide[...].reshape(BRICKS, 64, 128).astype(BF16)


def level_three(nb, own_in, low_in, high_in, bits, weights,
                out, own, low, high, cols, wide):
    fill(own, low, high, own_in, low_in, high_in)
    assemble(2, 256, nb, own, low, high, cols)

    def finish(half, first, sums):
        for p in range(sums.shape[0]):
            for b in range(BRICKS):
                at = b * 16 + (first + p) * 8
                mask = ((bits[at : at + 8, :] >> (4 * half)) & 15) != 0
                for part in range(2):
                    value = jnp.where(
                        mask, jnp.maximum(sums[p, b, :, 128 * part : 128 * part + 128], 0.0), 0.0
                    )
                    wide[part, pl.ds(8 * b + 4 * (first + p) + half, 2, stride=2), :] = value[0:2]

    convolve(2, 768, cols, lambda tap: weights[3 * tap : 3 * tap + 3].reshape(768, 256), finish)
    for part in range(2):
        out[:, :, 128 * part : 128 * part + 128] = wide[part].reshape(BRICKS, 8, 128).astype(BF16)


VM = pl.BlockSpec(memory_space=pltpu.VMEM)
SM = pl.BlockSpec(memory_space=pltpu.SMEM)


def call(body, outs, scratch, *args):
    return pl.pallas_call(
        body,
        out_shape=[jax.ShapeDtypeStruct(shape, dtype) for shape, dtype in outs],
        in_specs=[SM] + [VM] * (len(args) - 1),
        out_specs=[VM] * len(outs),
        scratch_shapes=[pltpu.VMEM(shape, dtype) for shape, dtype in scratch],
        compiler_params=pltpu.CompilerParams(vmem_limit_bytes=56 << 20),
    )(*args)


def exchange(first, last):
    count = lax.axis_size("morton")
    forward = [(i, i + 1) for i in range(count - 1)]
    low = lax.ppermute(last, "morton", forward)
    high = lax.ppermute(first, "morton", [(b, a) for a, b in forward])
    return low, high


def volume(side, width):
    return [
        ((BRICKS + 1, side * 8, LANES), F32),
        ((BRICKS + 1, 8, LANES), F32),
        ((BRICKS + 1, 8, LANES), F32),
        ((3, side + 2, 64, width), BF16),
    ]


def masked_plane(features, occupancy, plane):
    words = occupancy[:, 2 * plane : 2 * plane + 2]
    bits = (words[:, :, None] >> jnp.arange(32, dtype=jnp.int32)) & 1
    values = features[:, 64 * plane : 64 * plane + 64, :]
    return jnp.where(bits.reshape(BRICKS, 64, 1) != 0, values, jnp.zeros((), BF16))


def on_device(features, neighbours, occupancy, conv_one, first_reduce_kernel,
              conv_two, second_reduce_kernel, conv_three):
    low, high = exchange(
        masked_plane(features, occupancy, 0), masked_plane(features, occupancy, 7)
    )
    band = [((9, 512, 256), BF16)]
    first, own, to_low, to_high, bits = call(
        level_one,
        [(features.shape, BF16), ((BRICKS, 32, LANES), F32), ((BRICKS, 8, LANES), BF16),
         ((BRICKS, 8, LANES), BF16), ((BRICKS * 32, 128), jnp.int32)],
        volume(8, 768) + band + [((4, 528, 128), F32), ((512, 128), F32), ((512, 128), F32),
                                 ((512, 128), jnp.int32), ((272, 128), jnp.int32)],
        neighbours, features, occupancy, low, high, conv_one,
        first_reduce_kernel.reshape(512, 128),
    )
    low, high = exchange(to_low, to_high)
    second, own, to_low, to_high, bits = call(
        level_two,
        [((BRICKS, 64, 128), BF16), ((BRICKS, 16, LANES), F32), ((BRICKS, 8, LANES), BF16),
         ((BRICKS, 8, LANES), BF16), ((BRICKS * 16, 128), jnp.int32)],
        volume(4, 768) + band + [((4, 272, 128), F32), ((512, 128), F32), ((144, 128), jnp.int32)],
        neighbours, own, low, high, bits, conv_two, second_reduce_kernel.reshape(1024, 256),
    )
    low, high = exchange(to_low, to_high)
    (third,) = call(
        level_three,
        [((BRICKS, 8, 256), BF16)],
        volume(2, 1024) + [((2, 64, 128), F32)],
        neighbours, own, low, high, bits, conv_three,
    )
    return first, second, third


def solution(mesh):
    split = P(("tiles", "morton"), None, None)
    flat = P(("tiles", "morton"), None)
    return jax.shard_map(
        on_device,
        mesh=mesh,
        in_specs=(split, flat, flat, P(), P(), P(), P(), P()),
        out_specs=(split, split, split),
        check_vma=False,
    )
```

```python
import jax
import jax.numpy as jnp
from jax import lax
from jax.experimental import pallas as pl
from jax.experimental.pallas import tpu as pltpu
from jax.sharding import PartitionSpec as P

BRICKS = 8
LANES = 512
F32 = jnp.float32
BF16 = jnp.bfloat16


def iota(shape, dim):
    return lax.broadcasted_iota(jnp.int32, shape, dim)


def band_pairs(source, band):
    @pl.loop(0, 9)
    def _(tap):
        minus, same, plus = (source[3 * tap + e] for e in range(3))
        zero = jnp.zeros_like(same)
        low = jnp.concatenate([same, minus], axis=1)
        high = jnp.concatenate([plus, same], axis=1)
        before = jnp.concatenate([minus, zero], axis=1)
        after = jnp.concatenate([zero, plus], axis=1)
        blank = jnp.zeros((64, 128), BF16)
        rows = (
            (blank, blank), (before, blank),
            (low, blank), (high, before),
            (after, low), (blank, high),
            (blank, after), (blank, blank),
        )
        for at, (left, right) in enumerate(rows):
            band[tap, at * 64 : at * 64 + 64, 0:128] = left
            band[tap, at * 64 : at * 64 + 64, 128:256] = right


def band_single(source, band):
    @pl.loop(0, 9)
    def _(tap):
        minus, same, plus = (source[3 * tap + e] for e in range(3))
        blank = jnp.zeros_like(same)
        rows = ((minus, blank), (same, minus), (plus, same), (blank, plus))
        for at, (left, right) in enumerate(rows):
            band[tap, at * 128 : at * 128 + 128, 0:128] = left
            band[tap, at * 128 : at * 128 + 128, 128:256] = right


def assemble(side, halo, nb, sources, cols):
    row = iota((8, LANES + 2 * halo), 0)

    def source(brick, tap):
        number = nb[brick, tap]
        return jnp.where(number < 0, BRICKS, lax.rem(number, BRICKS))

    @pl.loop(0, BRICKS // 2)
    def _(pair):
        for dx, ref in sources:
            index = [
                [[source(2 * pair + b, 9 * dx + 3 * dy + dz) for dz in range(3)] for dy in range(3)]
                for b in range(2)
            ]
            for plane in range(side if dx == 1 else 1):
                at = slice(8 * plane, 8 * plane + 8)
                shifted = [[], [], []]
                for b in range(2):
                    views = []
                    for dy in range(3):
                        before, here, after = index[b][dy]
                        views.append(
                            jnp.concatenate(
                                [
                                    ref[before, at, LANES - halo : LANES],
                                    ref[here, at, :],
                                    ref[after, at, 0:halo],
                                ],
                                axis=1,
                            )
                        )
                    back, mid, front = views
                    shifted[0].append(
                        jnp.where(
                            row == 0,
                            pltpu.roll(back, (9 - side) % 8, 0),
                            pltpu.roll(mid, 1, 0),
                        )
                    )
                    shifted[1].append(mid)
                    shifted[2].append(
                        jnp.where(
                            row == side - 1,
                            pltpu.roll(front, side - 1, 0),
                            pltpu.roll(mid, 7, 0),
                        )
                    )
                to = plane + 1 if dx == 1 else (0 if dx == 0 else side + 1)
                rows = pl.ds(pl.multiple_of(16 * pair, 16), 16)
                for c in range(3):
                    cols[c, to, rows, :] = jnp.concatenate(shifted[c], axis=0).astype(BF16)


def convolve(side, depth, cols, weights, finish):
    chunk = min(side, 4)
    matrix = jnp.concatenate([weights(tap) for tap in range(9)], axis=0)
    for half in range(2):
        lanes = slice(256 * half, 256 * half + depth)
        for first in range(0, side, chunk):
            left = jnp.concatenate(
                [
                    cols[c, first + a : first + a + chunk, :, lanes].reshape(chunk * 64, depth)
                    for a in range(3)
                    for c in range(3)
                ],
                axis=1,
            )
            sums = jnp.dot(left, matrix, preferred_element_type=F32)
            finish(half, first, sums.reshape(chunk, BRICKS, 8, 256))


def rounded(value):
    return value.astype(BF16).astype(F32)


def pool_bits(bits, fine_side, temp, pooled):
    half = fine_side // 2
    count = BRICKS * half * 8
    joined = bits[0 : BRICKS * fine_side * 8, :].reshape(BRICKS * half, 2, 8, 128)
    temp[0:count, :] = (joined[:, 0] | joined[:, 1]).reshape(count, 128)
    temp[count : count + 16, :] = jnp.zeros((16, 128), jnp.int32)
    for at in range(BRICKS * half):
        even = temp[pl.ds(8 * at, 8, stride=2), :]
        odd = temp[pl.ds(8 * at + 1, 8, stride=2), :]
        pooled[8 * at : 8 * at + 8, :] = even | odd


def reduce_level(side, block, fine, kernel, bits, bit_width, emit):
    half = side // 2
    width = 2 * block
    for at in range(LANES // width):
        parts = []
        for ci in range(2):
            for cj in range(2):
                pieces = []
                for lane in range(at * width, (at + 1) * width, 128):
                    pieces.append(
                        jnp.concatenate(
                            [
                                fine[lane // 128, pl.ds((b * side + 2 * i + ci) * 8 + cj, 8, stride=2), :]
                                for b in range(BRICKS)
                                for i in range(half)
                            ],
                            axis=0,
                        )
                    )
                parts += pieces
        left = jnp.concatenate(parts, axis=1).astype(BF16)
        sums = jnp.dot(left, kernel, preferred_element_type=F32)
        mask = ((bits[0 : BRICKS * half * 8, :] >> (bit_width * at)) & ((1 << bit_width) - 1)) != 0
        wide = sums.shape[1]
        for lane in range(0, wide, 128):
            emit(
                at * wide + lane,
                jnp.where(mask, jnp.maximum(sums[:, lane : lane + 128], 0.0), 0.0),
            )


def relayout(temp, lane):
    for q in range(4):
        even = temp[pl.ds(2 * q, 64, stride=8), :]
        odd = temp[pl.ds(2 * q + 1, 64, stride=8), :]
        yield q, jnp.where(lane < 64, even, pltpu.roll(odd, 64, 1))


def fused(nb, feat, occ, conv_one, kernel_one, conv_two_hbm, kernel_two_hbm, conv_three_hbm,
          out_one, out_two, out_three,
          own_one, own_two, own_three, low, high, cols_one, cols_two, cols_three,
          band_one, band_two, conv_two, kernel_two, conv_three,
          fine, temp, wide, wide_three, bits_one, bits_two, bits_three, bits_temp,
          outgoing, incoming, load_sems, send_sems, recv_sems):
    me = lax.axis_index("morton")
    count = lax.axis_size("morton")
    has_low, has_high = me > 0, me < count - 1
    sides = ((has_low, me - 1), (has_high, me + 1))

    loads = [
        pltpu.make_async_copy(source, target, load_sems.at[at])
        for at, (source, target) in enumerate(
            ((conv_two_hbm, conv_two), (kernel_two_hbm, kernel_two), (conv_three_hbm, conv_three))
        )
    ]
    for load in loads:
        load.start()

    barrier = pltpu.get_barrier_semaphore()
    for there, device in sides:
        @pl.when(there)
        def _():
            pl.semaphore_signal(barrier, inc=1, device_id={"morton": device},
                                device_id_type=pl.DeviceIdType.MESH)

    def transfer(level, to):
        return pltpu.make_async_remote_copy(
            src_ref=outgoing.at[level, to],
            dst_ref=incoming.at[level, 1 - to],
            send_sem=send_sems.at[level, to],
            recv_sem=recv_sems.at[level, 1 - to],
            device_id={"morton": sides[to][1]},
            device_id_type=pl.DeviceIdType.MESH,
        )

    def send(level):
        for to in range(2):
            @pl.when(sides[to][0])
            def _():
                transfer(level, to).start()

    def receive(level):
        for source in range(2):
            @pl.when(sides[source][0])
            def _():
                transfer(level, 1 - source).wait_recv()
                (low, high)[source][0:BRICKS] = incoming[level, source].astype(F32)

    lane = iota((64, 128), 1)
    row = iota((64, 16), 0)
    column = iota((64, 16), 1)
    upper = (lane >= 64).astype(jnp.int32)
    for ref in (own_one, own_two, own_three):
        ref[BRICKS] = jnp.zeros(ref.shape[1:], F32)
    for ref in (low, high):
        ref[...] = jnp.zeros(ref.shape, F32)

    @pl.loop(0, BRICKS)
    def _(b):
        words = jnp.broadcast_to(occ[pl.ds(b, 1), :], (64, 16))
        octet = (words >> (8 * (row % 4))) & 255
        picked = jnp.where(column == row // 4, octet.astype(F32), 0.0)
        mask = jnp.broadcast_to(jnp.sum(picked, axis=1, keepdims=True), (64, 128)).astype(jnp.int32)
        bits_one[pl.ds(pl.multiple_of(64 * b, 64), 64), :] = mask
        temp[:, 0:64] = feat[b].astype(F32)
        for q, both in relayout(temp, lane):
            value = jnp.where(((mask >> (2 * q + upper)) & 1) != 0, both, 0.0)
            lanes = slice(128 * q, 128 * q + 128)
            own_one[b, :, lanes] = value
            outgoing[0, 0, b, :, lanes] = value[0:8].astype(BF16)
            outgoing[0, 1, b, :, lanes] = value[56:64].astype(BF16)

    pl.semaphore_wait(barrier, jnp.minimum(me, 1) + jnp.minimum(count - 1 - me, 1))
    send(0)
    band_pairs(conv_one, band_one)
    assemble(8, 128, nb, ((1, own_one),), cols_one)
    loads[0].wait()
    band_single(conv_two, band_two)
    receive(0)
    assemble(8, 128, nb, ((0, low), (2, high)), cols_one)

    small_upper = (iota((8, 128), 1) >= 64).astype(jnp.int32)

    def finish_one(half, first, sums):
        for p in range(sums.shape[0]):
            for b in range(BRICKS):
                at = b * 64 + (first + p) * 8
                mask = bits_one[at : at + 8, :]
                for part in range(2):
                    q = 2 * half + part
                    fine[q, at : at + 8, :] = rounded(
                        jnp.where(
                            ((mask >> (2 * q + small_upper)) & 1) != 0,
                            jnp.maximum(sums[p, b, :, 128 * part : 128 * part + 128], 0.0),
                            0.0,
                        )
                    )

    convolve(8, 512, cols_one, lambda tap: band_one[tap], finish_one)
    fine[:, 512:528, :] = jnp.zeros((4, 16, 128), F32)
    pool_bits(bits_one, 8, bits_temp, bits_two)

    def emit_into(own, level, planes):
        def emit(lane_at, value):
            value = rounded(value).reshape(BRICKS, 8 * planes, 128)
            lanes = slice(lane_at, lane_at + 128)
            own[0:BRICKS, :, lanes] = value
            outgoing[level, 0, :, :, lanes] = value[:, 0:8].astype(BF16)
            outgoing[level, 1, :, :, lanes] = value[:, 8 * planes - 8 :].astype(BF16)
        return emit

    reduce_level(8, 64, fine, kernel_one[...], bits_two, 2, emit_into(own_two, 1, 4))
    send(1)
    assemble(4, 128, nb, ((1, own_two),), cols_two)

    @pl.loop(0, BRICKS)
    def _(b):
        for q in range(4):
            both = fine[q, pl.ds(pl.multiple_of(64 * b, 64), 64), :]
            wide[pl.ds(2 * q, 64, stride=8), :] = both
            wide[pl.ds(2 * q + 1, 64, stride=8), :] = pltpu.roll(both, 64, 1)
        out_one[b] = wide[:, 0:64].astype(BF16)

    receive(1)
    assemble(4, 128, nb, ((0, low), (2, high)), cols_two)

    def finish_two(half, first, sums):
        for p in range(sums.shape[0]):
            for b in range(BRICKS):
                at = b * 32 + (first + p) * 8
                mask = bits_two[at : at + 8, :]
                for part in range(2):
                    q = 2 * half + part
                    fine[q, at : at + 8, :] = rounded(
                        jnp.where(
                            ((mask >> (2 * q)) & 3) != 0,
                            jnp.maximum(sums[p, b, :, 128 * part : 128 * part + 128], 0.0),
                            0.0,
                        )
                    )

    convolve(4, 512, cols_two, lambda tap: band_two[tap], finish_two)
    pool_bits(bits_two, 4, bits_temp, bits_three)
    loads[1].wait()
    reduce_level(4, 128, fine, kernel_two[...], bits_three, 4, emit_into(own_three, 2, 2))
    send(2)
    assemble(2, 256, nb, ((1, own_three),), cols_three)
    for b in range(BRICKS):
        for i in range(4):
            for k in range(4):
                at = b * 32 + 8 * i
                wide[pl.ds(64 * b + 16 * i + k, 4, stride=4), :] = fine[k, at : at + 4, :]
    out_two[...] = wide[...].reshape(BRICKS, 64, 128).astype(BF16)
    loads[2].wait()
    receive(2)
    assemble(2, 256, nb, ((0, low), (2, high)), cols_three)

    def finish_three(half, first, sums):
        for p in range(sums.shape[0]):
            for b in range(BRICKS):
                at = b * 16 + (first + p) * 8
                mask = ((bits_three[at : at + 8, :] >> (4 * half)) & 15) != 0
                for part in range(2):
                    value = jnp.where(
                        mask, jnp.maximum(sums[p, b, :, 128 * part : 128 * part + 128], 0.0), 0.0
                    )
                    wide_three[part, pl.ds(8 * b + 4 * (first + p) + half, 2, stride=2), :] = value[0:2]

    convolve(2, 768, cols_three, lambda tap: conv_three[3 * tap : 3 * tap + 3].reshape(768, 256), finish_three)
    for part in range(2):
        out_three[:, :, 128 * part : 128 * part + 128] = (
            wide_three[part].reshape(BRICKS, 8, 128).astype(BF16)
        )
    for level in range(3):
        for to in range(2):
            @pl.when(sides[to][0])
            def _():
                transfer(level, to).wait_send()


def on_device(features, neighbours, occupancy, conv_one, first_reduce_kernel,
              conv_two, second_reduce_kernel, conv_three):
    vm = pl.BlockSpec(memory_space=pltpu.VMEM)
    hbm = pl.BlockSpec(memory_space=pl.ANY)
    kernel_two = second_reduce_kernel.reshape(1024, 256)
    scratch = [
        ((BRICKS + 1, 64, LANES), F32), ((BRICKS + 1, 32, LANES), F32),
        ((BRICKS + 1, 16, LANES), F32), ((BRICKS + 1, 8, LANES), F32),
        ((BRICKS + 1, 8, LANES), F32),
        ((3, 10, 64, 768), BF16), ((3, 6, 64, 768), BF16), ((3, 4, 64, 1024), BF16),
        ((9, 512, 256), BF16), ((9, 512, 256), BF16),
        (conv_two.shape, BF16), (kernel_two.shape, BF16), (conv_three.shape, BF16),
        ((4, 528, 128), F32), ((512, 128), F32), ((512, 128), F32), ((2, 64, 128), F32),
        ((512, 128), jnp.int32), ((256, 128), jnp.int32), ((128, 128), jnp.int32),
        ((272, 128), jnp.int32),
        ((3, 2, BRICKS, 8, LANES), BF16), ((3, 2, BRICKS, 8, LANES), BF16),
    ]
    return pl.pallas_call(
        fused,
        out_shape=[
            jax.ShapeDtypeStruct((BRICKS, 512, 64), BF16),
            jax.ShapeDtypeStruct((BRICKS, 64, 128), BF16),
            jax.ShapeDtypeStruct((BRICKS, 8, 256), BF16),
        ],
        in_specs=[pl.BlockSpec(memory_space=pltpu.SMEM), vm, vm, vm, vm, hbm, hbm, hbm],
        out_specs=[vm, vm, vm],
        scratch_shapes=[pltpu.VMEM(shape, dtype) for shape, dtype in scratch]
        + [pltpu.SemaphoreType.DMA((3,)), pltpu.SemaphoreType.DMA((3, 2)),
           pltpu.SemaphoreType.DMA((3, 2))],
        compiler_params=pltpu.CompilerParams(
            collective_id=0, has_side_effects=True, vmem_limit_bytes=56 << 20
        ),
    )(neighbours, features, occupancy, conv_one, first_reduce_kernel.reshape(512, 128),
      conv_two, kernel_two, conv_three)


def solution(mesh):
    split = P(("tiles", "morton"), None, None)
    flat = P(("tiles", "morton"), None)
    return jax.shard_map(
        on_device,
        mesh=mesh,
        in_specs=(split, flat, flat, P(), P(), P(), P(), P()),
        out_specs=(split, split, split),
        check_vma=False,
    )
```

```python
import jax
import jax.numpy as jnp
from jax import lax
from jax.experimental import pallas as pl
from jax.experimental.pallas import tpu as pltpu
from jax.sharding import PartitionSpec as P

BRICKS = 8
LANES = 512
F32 = jnp.float32
BF16 = jnp.bfloat16


def iota(shape, dim):
    return lax.broadcasted_iota(jnp.int32, shape, dim)


def band_pairs(source, band):
    @pl.loop(0, 9)
    def _(tap):
        minus, same, plus = (source[3 * tap + e] for e in range(3))
        zero = jnp.zeros_like(same)
        low = jnp.concatenate([same, minus], axis=1)
        high = jnp.concatenate([plus, same], axis=1)
        before = jnp.concatenate([minus, zero], axis=1)
        after = jnp.concatenate([zero, plus], axis=1)
        blank = jnp.zeros((64, 128), BF16)
        rows = (
            (blank, blank), (before, blank),
            (low, blank), (high, before),
            (after, low), (blank, high),
            (blank, after), (blank, blank),
        )
        for at, (left, right) in enumerate(rows):
            band[tap, at * 64 : at * 64 + 64, 0:128] = left
            band[tap, at * 64 : at * 64 + 64, 128:256] = right


def band_single(source, band):
    @pl.loop(0, 9)
    def _(tap):
        minus, same, plus = (source[3 * tap + e] for e in range(3))
        blank = jnp.zeros_like(same)
        rows = ((minus, blank), (same, minus), (plus, same), (blank, plus))
        for at, (left, right) in enumerate(rows):
            band[tap, at * 128 : at * 128 + 128, 0:128] = left
            band[tap, at * 128 : at * 128 + 128, 128:256] = right


def assemble(side, halo, nb, sources, cols):
    row = iota((8, LANES + 2 * halo), 0)

    def source(brick, tap):
        number = nb[brick, tap]
        return jnp.where(number < 0, BRICKS, lax.rem(number, BRICKS))

    @pl.loop(0, BRICKS // 2)
    def _(pair):
        for dx, ref in sources:
            index = [
                [[source(2 * pair + b, 9 * dx + 3 * dy + dz) for dz in range(3)] for dy in range(3)]
                for b in range(2)
            ]
            for plane in range(side if dx == 1 else 1):
                at = slice(8 * plane, 8 * plane + 8)
                shifted = [[], [], []]
                for b in range(2):
                    views = []
                    for dy in range(3):
                        before, here, after = index[b][dy]
                        views.append(
                            jnp.concatenate(
                                [
                                    ref[before, at, LANES - halo : LANES],
                                    ref[here, at, :],
                                    ref[after, at, 0:halo],
                                ],
                                axis=1,
                            )
                        )
                    back, mid, front = views
                    shifted[0].append(
                        jnp.where(
                            row == 0,
                            pltpu.roll(back, (9 - side) % 8, 0),
                            pltpu.roll(mid, 1, 0),
                        )
                    )
                    shifted[1].append(mid)
                    shifted[2].append(
                        jnp.where(
                            row == side - 1,
                            pltpu.roll(front, side - 1, 0),
                            pltpu.roll(mid, 7, 0),
                        )
                    )
                to = plane + 1 if dx == 1 else (0 if dx == 0 else side + 1)
                rows = pl.ds(pl.multiple_of(16 * pair, 16), 16)
                for c in range(3):
                    cols[c, to, rows, :] = jnp.concatenate(shifted[c], axis=0).astype(BF16)


def convolve(side, depth, cols, weights, finish):
    chunk = min(side, 4)
    matrix = jnp.concatenate([weights(tap) for tap in range(9)], axis=0)
    for half in range(2):
        lanes = slice(256 * half, 256 * half + depth)
        for first in range(0, side, chunk):
            left = jnp.concatenate(
                [
                    cols[c, first + a : first + a + chunk, :, lanes].reshape(chunk * 64, depth)
                    for a in range(3)
                    for c in range(3)
                ],
                axis=1,
            )
            sums = jnp.dot(left, matrix, preferred_element_type=F32)
            finish(half, first, sums.reshape(chunk, BRICKS, 8, 256))


def rounded(value):
    return value.astype(BF16).astype(F32)


def pool_bits(bits, fine_side, temp, pooled):
    half = fine_side // 2
    count = BRICKS * half * 8
    joined = bits[0 : BRICKS * fine_side * 8, :].reshape(BRICKS * half, 2, 8, 128)
    temp[0:count, :] = (joined[:, 0] | joined[:, 1]).reshape(count, 128)
    temp[count : count + 16, :] = jnp.zeros((16, 128), jnp.int32)
    for at in range(BRICKS * half):
        even = temp[pl.ds(8 * at, 8, stride=2), :]
        odd = temp[pl.ds(8 * at + 1, 8, stride=2), :]
        pooled[8 * at : 8 * at + 8, :] = even | odd


def reduce_level(side, block, fine, kernel, bits, bit_width, emit):
    half = side // 2
    width = 2 * block
    for at in range(LANES // width):
        parts = []
        for ci in range(2):
            for cj in range(2):
                pieces = []
                for lane in range(at * width, (at + 1) * width, 128):
                    pieces.append(
                        jnp.concatenate(
                            [
                                fine[lane // 128, pl.ds((b * side + 2 * i + ci) * 8 + cj, 8, stride=2), :]
                                for b in range(BRICKS)
                                for i in range(half)
                            ],
                            axis=0,
                        )
                    )
                parts += pieces
        left = jnp.concatenate(parts, axis=1).astype(BF16)
        sums = jnp.dot(left, kernel, preferred_element_type=F32)
        mask = ((bits[0 : BRICKS * half * 8, :] >> (bit_width * at)) & ((1 << bit_width) - 1)) != 0
        wide = sums.shape[1]
        for lane in range(0, wide, 128):
            emit(
                at * wide + lane,
                jnp.where(mask, jnp.maximum(sums[:, lane : lane + 128], 0.0), 0.0),
            )


def relayout(temp, lane):
    for q in range(4):
        even = temp[pl.ds(2 * q, 64, stride=8), :]
        odd = temp[pl.ds(2 * q + 1, 64, stride=8), :]
        yield q, jnp.where(lane < 64, even, pltpu.roll(odd, 64, 1))


def fused(nb, feat, occ, conv_one, kernel_one, conv_two_hbm, kernel_two_hbm, conv_three_hbm,
          out_one, out_two, out_three,
          own_one, own_two, own_three, low, high, cols_one, cols_two, cols_three,
          band_one, band_two, conv_two, kernel_two, conv_three,
          fine, temp, wide, wide_three, bits_one, bits_two, bits_three, bits_temp,
          outgoing, incoming, load_sems, send_sems, recv_sems):
    me = lax.axis_index("morton")
    count = lax.axis_size("morton")
    has_low, has_high = me > 0, me < count - 1
    sides = ((has_low, me - 1), (has_high, me + 1))

    loads = [
        pltpu.make_async_copy(source, target, load_sems.at[at])
        for at, (source, target) in enumerate(
            ((conv_two_hbm, conv_two), (kernel_two_hbm, kernel_two), (conv_three_hbm, conv_three))
        )
    ]
    for load in loads:
        load.start()

    barrier = pltpu.get_barrier_semaphore()
    for there, device in sides:
        @pl.when(there)
        def _():
            pl.semaphore_signal(barrier, inc=1, device_id={"morton": device},
                                device_id_type=pl.DeviceIdType.MESH)

    def transfer(level, to):
        return pltpu.make_async_remote_copy(
            src_ref=outgoing.at[level, to],
            dst_ref=incoming.at[level, 1 - to],
            send_sem=send_sems.at[level, to],
            recv_sem=recv_sems.at[level, 1 - to],
            device_id={"morton": sides[to][1]},
            device_id_type=pl.DeviceIdType.MESH,
        )

    def send(level):
        for to in range(2):
            @pl.when(sides[to][0])
            def _():
                transfer(level, to).start()

    def receive(level):
        for source in range(2):
            @pl.when(sides[source][0])
            def _():
                transfer(level, 1 - source).wait_recv()
                (low, high)[source][0:BRICKS] = incoming[level, source].astype(F32)

    lane = iota((64, 128), 1)
    row = iota((64, 16), 0)
    column = iota((64, 16), 1)
    upper = (lane >= 64).astype(jnp.int32)
    for ref in (own_one, own_two, own_three):
        ref[BRICKS] = jnp.zeros(ref.shape[1:], F32)
    for ref in (low, high):
        ref[...] = jnp.zeros(ref.shape, F32)

    @pl.loop(0, BRICKS)
    def _(b):
        words = jnp.broadcast_to(occ[pl.ds(b, 1), :], (64, 16))
        octet = (words >> (8 * (row % 4))) & 255
        picked = jnp.where(column == row // 4, octet.astype(F32), 0.0)
        mask = jnp.broadcast_to(jnp.sum(picked, axis=1, keepdims=True), (64, 128)).astype(jnp.int32)
        bits_one[pl.ds(pl.multiple_of(64 * b, 64), 64), :] = mask
        temp[:, 0:64] = feat[b].astype(F32).T
        for q, both in relayout(temp, lane):
            value = jnp.where(((mask >> (2 * q + upper)) & 1) != 0, both, 0.0)
            lanes = slice(128 * q, 128 * q + 128)
            own_one[b, :, lanes] = value
            outgoing[0, 0, b, :, lanes] = value[0:8].astype(BF16)
            outgoing[0, 1, b, :, lanes] = value[56:64].astype(BF16)

    pl.semaphore_wait(barrier, jnp.minimum(me, 1) + jnp.minimum(count - 1 - me, 1))
    send(0)
    band_pairs(conv_one, band_one)
    assemble(8, 128, nb, ((1, own_one),), cols_one)
    loads[0].wait()
    band_single(conv_two, band_two)
    receive(0)
    assemble(8, 128, nb, ((0, low), (2, high)), cols_one)

    small_upper = (iota((8, 128), 1) >= 64).astype(jnp.int32)

    def finish_one(half, first, sums):
        for p in range(sums.shape[0]):
            for b in range(BRICKS):
                at = b * 64 + (first + p) * 8
                mask = bits_one[at : at + 8, :]
                for part in range(2):
                    q = 2 * half + part
                    fine[q, at : at + 8, :] = rounded(
                        jnp.where(
                            ((mask >> (2 * q + small_upper)) & 1) != 0,
                            jnp.maximum(sums[p, b, :, 128 * part : 128 * part + 128], 0.0),
                            0.0,
                        )
                    )

    convolve(8, 512, cols_one, lambda tap: band_one[tap], finish_one)
    fine[:, 512:528, :] = jnp.zeros((4, 16, 128), F32)
    pool_bits(bits_one, 8, bits_temp, bits_two)

    def emit_into(own, level, planes):
        def emit(lane_at, value):
            value = rounded(value).reshape(BRICKS, 8 * planes, 128)
            lanes = slice(lane_at, lane_at + 128)
            own[0:BRICKS, :, lanes] = value
            outgoing[level, 0, :, :, lanes] = value[:, 0:8].astype(BF16)
            outgoing[level, 1, :, :, lanes] = value[:, 8 * planes - 8 :].astype(BF16)
        return emit

    reduce_level(8, 64, fine, kernel_one[...], bits_two, 2, emit_into(own_two, 1, 4))
    send(1)
    assemble(4, 128, nb, ((1, own_two),), cols_two)

    @pl.loop(0, BRICKS)
    def _(b):
        for q in range(4):
            both = fine[q, pl.ds(pl.multiple_of(64 * b, 64), 64), :]
            wide[pl.ds(2 * q, 64, stride=8), :] = both
            wide[pl.ds(2 * q + 1, 64, stride=8), :] = pltpu.roll(both, 64, 1)
        out_one[b] = wide[:, 0:64].T.astype(BF16)

    receive(1)
    assemble(4, 128, nb, ((0, low), (2, high)), cols_two)

    def finish_two(half, first, sums):
        for p in range(sums.shape[0]):
            for b in range(BRICKS):
                at = b * 32 + (first + p) * 8
                mask = bits_two[at : at + 8, :]
                for part in range(2):
                    q = 2 * half + part
                    fine[q, at : at + 8, :] = rounded(
                        jnp.where(
                            ((mask >> (2 * q)) & 3) != 0,
                            jnp.maximum(sums[p, b, :, 128 * part : 128 * part + 128], 0.0),
                            0.0,
                        )
                    )

    convolve(4, 512, cols_two, lambda tap: band_two[tap], finish_two)
    pool_bits(bits_two, 4, bits_temp, bits_three)
    loads[1].wait()
    reduce_level(4, 128, fine, kernel_two[...], bits_three, 4, emit_into(own_three, 2, 2))
    send(2)
    assemble(2, 256, nb, ((1, own_three),), cols_three)
    for b in range(BRICKS):
        for i in range(4):
            for k in range(4):
                at = b * 32 + 8 * i
                wide[pl.ds(64 * b + 16 * i + k, 4, stride=4), :] = fine[k, at : at + 4, :]
    out_two[...] = wide[...].reshape(BRICKS, 64, 128).astype(BF16)
    loads[2].wait()
    receive(2)
    assemble(2, 256, nb, ((0, low), (2, high)), cols_three)

    def finish_three(half, first, sums):
        for p in range(sums.shape[0]):
            for b in range(BRICKS):
                at = b * 16 + (first + p) * 8
                mask = ((bits_three[at : at + 8, :] >> (4 * half)) & 15) != 0
                for part in range(2):
                    value = jnp.where(
                        mask, jnp.maximum(sums[p, b, :, 128 * part : 128 * part + 128], 0.0), 0.0
                    )
                    wide_three[part, pl.ds(8 * b + 4 * (first + p) + half, 2, stride=2), :] = value[0:2]

    convolve(2, 768, cols_three, lambda tap: conv_three[3 * tap : 3 * tap + 3].reshape(768, 256), finish_three)
    for part in range(2):
        out_three[:, :, 128 * part : 128 * part + 128] = (
            wide_three[part].reshape(BRICKS, 8, 128).astype(BF16)
        )
    for level in range(3):
        for to in range(2):
            @pl.when(sides[to][0])
            def _():
                transfer(level, to).wait_send()


def on_device(features, neighbours, occupancy, conv_one, first_reduce_kernel,
              conv_two, second_reduce_kernel, conv_three):
    vm = pl.BlockSpec(memory_space=pltpu.VMEM)
    hbm = pl.BlockSpec(memory_space=pl.ANY)
    kernel_two = second_reduce_kernel.reshape(1024, 256)
    scratch = [
        ((BRICKS + 1, 64, LANES), F32), ((BRICKS + 1, 32, LANES), F32),
        ((BRICKS + 1, 16, LANES), F32), ((BRICKS + 1, 8, LANES), F32),
        ((BRICKS + 1, 8, LANES), F32),
        ((3, 10, 64, 768), BF16), ((3, 6, 64, 768), BF16), ((3, 4, 64, 1024), BF16),
        ((9, 512, 256), BF16), ((9, 512, 256), BF16),
        (conv_two.shape, BF16), (kernel_two.shape, BF16), (conv_three.shape, BF16),
        ((4, 528, 128), F32), ((512, 128), F32), ((512, 128), F32), ((2, 64, 128), F32),
        ((512, 128), jnp.int32), ((256, 128), jnp.int32), ((128, 128), jnp.int32),
        ((272, 128), jnp.int32),
        ((3, 2, BRICKS, 8, LANES), BF16), ((3, 2, BRICKS, 8, LANES), BF16),
    ]
    first, second, third = pl.pallas_call(
        fused,
        out_shape=[
            jax.ShapeDtypeStruct((BRICKS, 64, 512), BF16),
            jax.ShapeDtypeStruct((BRICKS, 64, 128), BF16),
            jax.ShapeDtypeStruct((BRICKS, 8, 256), BF16),
        ],
        in_specs=[pl.BlockSpec(memory_space=pltpu.SMEM), vm, vm, vm, vm, hbm, hbm, hbm],
        out_specs=[vm, vm, vm],
        scratch_shapes=[pltpu.VMEM(shape, dtype) for shape, dtype in scratch]
        + [pltpu.SemaphoreType.DMA((3,)), pltpu.SemaphoreType.DMA((3, 2)),
           pltpu.SemaphoreType.DMA((3, 2))],
        compiler_params=pltpu.CompilerParams(
            collective_id=0, has_side_effects=True, vmem_limit_bytes=56 << 20
        ),
    )(neighbours, jnp.swapaxes(features, 1, 2), occupancy, conv_one, first_reduce_kernel.reshape(512, 128),
      conv_two, kernel_two, conv_three)
    return jnp.swapaxes(first, 1, 2), second, third


def solution(mesh):
    split = P(("tiles", "morton"), None, None)
    flat = P(("tiles", "morton"), None)
    return jax.shard_map(
        on_device,
        mesh=mesh,
        in_specs=(split, flat, flat, P(), P(), P(), P(), P()),
        out_specs=(split, split, split),
        check_vma=False,
    )
```

```python
import jax
import jax.numpy as jnp
from jax import lax
from jax.experimental import pallas as pl
from jax.experimental.pallas import tpu as pltpu
from jax.sharding import PartitionSpec as P

BRICKS = 8
LANES = 512
F32 = jnp.float32
BF16 = jnp.bfloat16


def iota(shape, dim):
    return lax.broadcasted_iota(jnp.int32, shape, dim)


def band_pairs(source, band):
    @pl.loop(0, 9)
    def _(tap):
        minus, same, plus = (source[3 * tap + e] for e in range(3))
        zero = jnp.zeros_like(same)
        low = jnp.concatenate([same, minus], axis=1)
        high = jnp.concatenate([plus, same], axis=1)
        before = jnp.concatenate([minus, zero], axis=1)
        after = jnp.concatenate([zero, plus], axis=1)
        blank = jnp.zeros((64, 128), BF16)
        rows = (
            (blank, blank), (before, blank),
            (low, blank), (high, before),
            (after, low), (blank, high),
            (blank, after), (blank, blank),
        )
        for at, (left, right) in enumerate(rows):
            band[tap, at * 64 : at * 64 + 64, 0:128] = left
            band[tap, at * 64 : at * 64 + 64, 128:256] = right


def band_single(source, band):
    @pl.loop(0, 9)
    def _(tap):
        minus, same, plus = (source[3 * tap + e] for e in range(3))
        blank = jnp.zeros_like(same)
        rows = ((minus, blank), (same, minus), (plus, same), (blank, plus))
        for at, (left, right) in enumerate(rows):
            band[tap, at * 128 : at * 128 + 128, 0:128] = left
            band[tap, at * 128 : at * 128 + 128, 128:256] = right


def assemble(side, halo, nb, sources, cols):
    row = iota((8, LANES + 2 * halo), 0)

    def source(brick, tap):
        number = nb[brick, tap]
        return jnp.where(number < 0, BRICKS, lax.rem(number, BRICKS))

    @pl.loop(0, BRICKS // 2)
    def _(pair):
        for dx, ref in sources:
            index = [
                [[source(2 * pair + b, 9 * dx + 3 * dy + dz) for dz in range(3)] for dy in range(3)]
                for b in range(2)
            ]
            for plane in range(side if dx == 1 else 1):
                at = slice(8 * plane, 8 * plane + 8)
                shifted = [[], [], []]
                for b in range(2):
                    views = []
                    for dy in range(3):
                        before, here, after = index[b][dy]
                        views.append(
                            jnp.concatenate(
                                [
                                    ref[before, at, LANES - halo : LANES],
                                    ref[here, at, :],
                                    ref[after, at, 0:halo],
                                ],
                                axis=1,
                            )
                        )
                    back, mid, front = views
                    shifted[0].append(
                        jnp.where(
                            row == 0,
                            pltpu.roll(back, (9 - side) % 8, 0),
                            pltpu.roll(mid, 1, 0),
                        )
                    )
                    shifted[1].append(mid)
                    shifted[2].append(
                        jnp.where(
                            row == side - 1,
                            pltpu.roll(front, side - 1, 0),
                            pltpu.roll(mid, 7, 0),
                        )
                    )
                to = plane + 1 if dx == 1 else (0 if dx == 0 else side + 1)
                rows = pl.ds(pl.multiple_of(16 * pair, 16), 16)
                for c in range(3):
                    cols[c, to, rows, :] = jnp.concatenate(shifted[c], axis=0).astype(BF16)


def convolve(side, depth, cols, weights, finish):
    chunk = min(side, 4)
    matrix = jnp.concatenate([weights(tap) for tap in range(9)], axis=0)
    for half in range(2):
        lanes = slice(256 * half, 256 * half + depth)
        for first in range(0, side, chunk):
            left = jnp.concatenate(
                [
                    cols[c, first + a : first + a + chunk, :, lanes].reshape(chunk * 64, depth)
                    for a in range(3)
                    for c in range(3)
                ],
                axis=1,
            )
            sums = jnp.dot(left, matrix, preferred_element_type=F32)
            finish(half, first, sums.reshape(chunk, BRICKS, 8, 256))


def rounded(value):
    return value.astype(BF16).astype(F32)


def pool_bits(bits, fine_side, temp, pooled):
    half = fine_side // 2
    count = BRICKS * half * 8
    joined = bits[0 : BRICKS * fine_side * 8, :].reshape(BRICKS * half, 2, 8, 128)
    temp[0:count, :] = (joined[:, 0] | joined[:, 1]).reshape(count, 128)
    temp[count : count + 16, :] = jnp.zeros((16, 128), jnp.int32)
    for at in range(BRICKS * half):
        even = temp[pl.ds(8 * at, 8, stride=2), :]
        odd = temp[pl.ds(8 * at + 1, 8, stride=2), :]
        pooled[8 * at : 8 * at + 8, :] = even | odd


def reduce_level(side, block, fine, kernel, bits, bit_width, emit):
    half = side // 2
    width = 2 * block
    for at in range(LANES // width):
        parts = []
        for ci in range(2):
            for cj in range(2):
                pieces = []
                for lane in range(at * width, (at + 1) * width, 128):
                    pieces.append(
                        jnp.concatenate(
                            [
                                fine[lane // 128, pl.ds((b * side + 2 * i + ci) * 8 + cj, 8, stride=2), :]
                                for b in range(BRICKS)
                                for i in range(half)
                            ],
                            axis=0,
                        )
                    )
                parts += pieces
        left = jnp.concatenate(parts, axis=1).astype(BF16)
        sums = jnp.dot(left, kernel, preferred_element_type=F32)
        mask = ((bits[0 : BRICKS * half * 8, :] >> (bit_width * at)) & ((1 << bit_width) - 1)) != 0
        wide = sums.shape[1]
        for lane in range(0, wide, 128):
            emit(
                at * wide + lane,
                jnp.where(mask, jnp.maximum(sums[:, lane : lane + 128], 0.0), 0.0),
            )


def relayout(temp, lane):
    for q in range(4):
        even = temp[pl.ds(2 * q, 64, stride=8), :]
        odd = temp[pl.ds(2 * q + 1, 64, stride=8), :]
        yield q, jnp.where(lane < 64, even, pltpu.roll(odd, 64, 1))


def fused(nb, feat, occ, conv_one, kernel_one, conv_two_hbm, kernel_two_hbm, conv_three_hbm,
          out_one, out_two, cols_three, bits_three, conv_three,
          own_one, own_two, own_three, low, high, cols_one, cols_two,
          band_one, band_two, conv_two, kernel_two,
          fine, temp, wide, bits_one, bits_two, bits_temp,
          outgoing, incoming, load_sems, send_sems, recv_sems):
    me = lax.axis_index("morton")
    count = lax.axis_size("morton")
    has_low, has_high = me > 0, me < count - 1
    sides = ((has_low, me - 1), (has_high, me + 1))

    loads = [
        pltpu.make_async_copy(source, target, load_sems.at[at])
        for at, (source, target) in enumerate(
            ((conv_two_hbm, conv_two), (kernel_two_hbm, kernel_two), (conv_three_hbm, conv_three))
        )
    ]
    for load in loads:
        load.start()

    barrier = pltpu.get_barrier_semaphore()
    for there, device in sides:
        @pl.when(there)
        def _():
            pl.semaphore_signal(barrier, inc=1, device_id={"morton": device},
                                device_id_type=pl.DeviceIdType.MESH)

    def transfer(level, to):
        return pltpu.make_async_remote_copy(
            src_ref=outgoing.at[level, to],
            dst_ref=incoming.at[level, 1 - to],
            send_sem=send_sems.at[level, to],
            recv_sem=recv_sems.at[level, 1 - to],
            device_id={"morton": sides[to][1]},
            device_id_type=pl.DeviceIdType.MESH,
        )

    def send(level):
        for to in range(2):
            @pl.when(sides[to][0])
            def _():
                transfer(level, to).start()

    def receive(level):
        for source in range(2):
            @pl.when(sides[source][0])
            def _():
                transfer(level, 1 - source).wait_recv()
                (low, high)[source][0:BRICKS] = incoming[level, source].astype(F32)

    lane = iota((64, 128), 1)
    row = iota((64, 16), 0)
    column = iota((64, 16), 1)
    upper = (lane >= 64).astype(jnp.int32)
    for ref in (own_one, own_two, own_three):
        ref[BRICKS] = jnp.zeros(ref.shape[1:], F32)
    for ref in (low, high):
        ref[...] = jnp.zeros(ref.shape, F32)

    @pl.loop(0, BRICKS)
    def _(b):
        words = jnp.broadcast_to(occ[pl.ds(b, 1), :], (64, 16))
        octet = (words >> (8 * (row % 4))) & 255
        picked = jnp.where(column == row // 4, octet.astype(F32), 0.0)
        mask = jnp.broadcast_to(jnp.sum(picked, axis=1, keepdims=True), (64, 128)).astype(jnp.int32)
        bits_one[pl.ds(pl.multiple_of(64 * b, 64), 64), :] = mask
        temp[:, 0:64] = feat[b].astype(F32).T
        for q, both in relayout(temp, lane):
            value = jnp.where(((mask >> (2 * q + upper)) & 1) != 0, both, 0.0)
            lanes = slice(128 * q, 128 * q + 128)
            own_one[b, :, lanes] = value
            outgoing[0, 0, b, :, lanes] = value[0:8].astype(BF16)
            outgoing[0, 1, b, :, lanes] = value[56:64].astype(BF16)

    pl.semaphore_wait(barrier, jnp.minimum(me, 1) + jnp.minimum(count - 1 - me, 1))
    send(0)
    band_pairs(conv_one, band_one)
    assemble(8, 128, nb, ((1, own_one),), cols_one)
    loads[0].wait()
    band_single(conv_two, band_two)
    receive(0)
    assemble(8, 128, nb, ((0, low), (2, high)), cols_one)

    small_upper = (iota((8, 128), 1) >= 64).astype(jnp.int32)

    def finish_one(half, first, sums):
        for p in range(sums.shape[0]):
            for b in range(BRICKS):
                at = b * 64 + (first + p) * 8
                mask = bits_one[at : at + 8, :]
                for part in range(2):
                    q = 2 * half + part
                    fine[q, at : at + 8, :] = rounded(
                        jnp.where(
                            ((mask >> (2 * q + small_upper)) & 1) != 0,
                            jnp.maximum(sums[p, b, :, 128 * part : 128 * part + 128], 0.0),
                            0.0,
                        )
                    )

    convolve(8, 512, cols_one, lambda tap: band_one[tap], finish_one)
    fine[:, 512:528, :] = jnp.zeros((4, 16, 128), F32)
    pool_bits(bits_one, 8, bits_temp, bits_two)

    def emit_into(own, level, planes):
        def emit(lane_at, value):
            value = rounded(value).reshape(BRICKS, 8 * planes, 128)
            lanes = slice(lane_at, lane_at + 128)
            own[0:BRICKS, :, lanes] = value
            outgoing[level, 0, :, :, lanes] = value[:, 0:8].astype(BF16)
            outgoing[level, 1, :, :, lanes] = value[:, 8 * planes - 8 :].astype(BF16)
        return emit

    reduce_level(8, 64, fine, kernel_one[...], bits_two, 2, emit_into(own_two, 1, 4))
    send(1)
    assemble(4, 128, nb, ((1, own_two),), cols_two)

    @pl.loop(0, BRICKS)
    def _(b):
        for q in range(4):
            both = fine[q, pl.ds(pl.multiple_of(64 * b, 64), 64), :]
            wide[pl.ds(2 * q, 64, stride=8), :] = both
            wide[pl.ds(2 * q + 1, 64, stride=8), :] = pltpu.roll(both, 64, 1)
        out_one[b] = wide[:, 0:64].T.astype(BF16)

    receive(1)
    assemble(4, 128, nb, ((0, low), (2, high)), cols_two)

    def finish_two(half, first, sums):
        for p in range(sums.shape[0]):
            for b in range(BRICKS):
                at = b * 32 + (first + p) * 8
                mask = bits_two[at : at + 8, :]
                for part in range(2):
                    q = 2 * half + part
                    fine[q, at : at + 8, :] = rounded(
                        jnp.where(
                            ((mask >> (2 * q)) & 3) != 0,
                            jnp.maximum(sums[p, b, :, 128 * part : 128 * part + 128], 0.0),
                            0.0,
                        )
                    )

    convolve(4, 512, cols_two, lambda tap: band_two[tap], finish_two)
    pool_bits(bits_two, 4, bits_temp, bits_three)
    loads[1].wait()
    reduce_level(4, 128, fine, kernel_two[...], bits_three, 4, emit_into(own_three, 2, 2))
    send(2)
    assemble(2, 256, nb, ((1, own_three),), cols_three)
    for b in range(BRICKS):
        for i in range(4):
            for k in range(4):
                at = b * 32 + 8 * i
                wide[pl.ds(64 * b + 16 * i + k, 4, stride=4), :] = fine[k, at : at + 4, :]
    out_two[...] = wide[...].reshape(BRICKS, 64, 128).astype(BF16)
    receive(2)
    assemble(2, 256, nb, ((0, low), (2, high)), cols_three)

    loads[2].wait()
    for level in range(3):
        for to in range(2):
            @pl.when(sides[to][0])
            def _():
                transfer(level, to).wait_send()


def last_level(one, two, cols_three, bits_three, conv_three,
               out_one, out_two, out_three, wide_three):
    out_one[...] = one[...]
    out_two[...] = two[...]

    def finish_three(half, first, sums):
        for p in range(sums.shape[0]):
            for b in range(BRICKS):
                at = b * 16 + (first + p) * 8
                mask = ((bits_three[at : at + 8, :] >> (4 * half)) & 15) != 0
                for part in range(2):
                    value = jnp.where(
                        mask, jnp.maximum(sums[p, b, :, 128 * part : 128 * part + 128], 0.0), 0.0
                    )
                    wide_three[part, pl.ds(8 * b + 4 * (first + p) + half, 2, stride=2), :] = value[0:2]

    convolve(2, 768, cols_three, lambda tap: conv_three[3 * tap : 3 * tap + 3].reshape(768, 256), finish_three)
    for part in range(2):
        out_three[:, :, 128 * part : 128 * part + 128] = (
            wide_three[part].reshape(BRICKS, 8, 128).astype(BF16)
        )


def on_device(features, neighbours, occupancy, conv_one, first_reduce_kernel,
              conv_two, second_reduce_kernel, conv_three):
    vm = pl.BlockSpec(memory_space=pltpu.VMEM)
    hbm = pl.BlockSpec(memory_space=pltpu.HBM)
    kernel_two = second_reduce_kernel.reshape(1024, 256)
    scratch = [
        ((BRICKS + 1, 64, LANES), F32), ((BRICKS + 1, 32, LANES), F32),
        ((BRICKS + 1, 16, LANES), F32), ((BRICKS + 1, 8, LANES), F32),
        ((BRICKS + 1, 8, LANES), F32),
        ((3, 10, 64, 768), BF16), ((3, 6, 64, 768), BF16),
        ((9, 512, 256), BF16), ((9, 512, 256), BF16),
        (conv_two.shape, BF16), (kernel_two.shape, BF16),
        ((4, 528, 128), F32), ((512, 128), F32), ((512, 128), F32),
        ((512, 128), jnp.int32), ((256, 128), jnp.int32),
        ((272, 128), jnp.int32),
        ((3, 2, BRICKS, 8, LANES), BF16), ((3, 2, BRICKS, 8, LANES), BF16),
    ]
    shapes = [
        jax.ShapeDtypeStruct((BRICKS, 64, 512), BF16),
        jax.ShapeDtypeStruct((BRICKS, 64, 128), BF16),
    ]
    first, second, cols, bits, weights = pl.pallas_call(
        fused,
        out_shape=shapes
        + [
            jax.ShapeDtypeStruct((3, 4, 64, 1024), BF16),
            jax.ShapeDtypeStruct((128, 128), jnp.int32),
            jax.ShapeDtypeStruct(conv_three.shape, BF16),
        ],
        in_specs=[pl.BlockSpec(memory_space=pltpu.SMEM), vm, vm, vm, vm, hbm, hbm, hbm],
        out_specs=[vm] * 5,
        scratch_shapes=[pltpu.VMEM(shape, dtype) for shape, dtype in scratch]
        + [pltpu.SemaphoreType.DMA((3,)), pltpu.SemaphoreType.DMA((3, 2)),
           pltpu.SemaphoreType.DMA((3, 2))],
        compiler_params=pltpu.CompilerParams(
            collective_id=0, has_side_effects=True, vmem_limit_bytes=36 << 20
        ),
    )(neighbours, jnp.swapaxes(features, 1, 2), occupancy, conv_one,
      first_reduce_kernel.reshape(512, 128), conv_two, kernel_two, conv_three)
    first, second, third = pl.pallas_call(
        last_level,
        out_shape=shapes + [jax.ShapeDtypeStruct((BRICKS, 8, 256), BF16)],
        in_specs=[vm] * 5,
        out_specs=[vm] * 3,
        scratch_shapes=[pltpu.VMEM((2, 64, 128), F32)],
        compiler_params=pltpu.CompilerParams(vmem_limit_bytes=16 << 20),
    )(first, second, cols, bits, weights)
    return jnp.swapaxes(first, 1, 2), second, third


def solution(mesh):
    split = P(("tiles", "morton"), None, None)
    flat = P(("tiles", "morton"), None)
    return jax.shard_map(
        on_device,
        mesh=mesh,
        in_specs=(split, flat, flat, P(), P(), P(), P(), P()),
        out_specs=(split, split, split),
        check_vma=False,
    )
```

```python
import jax
import jax.numpy as jnp
from jax import lax
from jax.experimental import pallas as pl
from jax.experimental.pallas import tpu as pltpu
from jax.sharding import PartitionSpec as P

BRICKS = 8
LANES = 512
F32 = jnp.float32
BF16 = jnp.bfloat16


def iota(shape, dim):
    return lax.broadcasted_iota(jnp.int32, shape, dim)


def band_pairs(source, band):
    @pl.loop(0, 9)
    def _(tap):
        minus, same, plus = (source[3 * tap + e] for e in range(3))
        zero = jnp.zeros_like(same)
        low = jnp.concatenate([same, minus], axis=1)
        high = jnp.concatenate([plus, same], axis=1)
        before = jnp.concatenate([minus, zero], axis=1)
        after = jnp.concatenate([zero, plus], axis=1)
        blank = jnp.zeros((64, 128), BF16)
        rows = (
            (blank, blank), (before, blank),
            (low, blank), (high, before),
            (after, low), (blank, high),
            (blank, after), (blank, blank),
        )
        for at, (left, right) in enumerate(rows):
            band[tap, at * 64 : at * 64 + 64, 0:128] = left
            band[tap, at * 64 : at * 64 + 64, 128:256] = right


def band_single(source, band):
    @pl.loop(0, 9)
    def _(tap):
        minus, same, plus = (source[3 * tap + e] for e in range(3))
        blank = jnp.zeros_like(same)
        rows = ((minus, blank), (same, minus), (plus, same), (blank, plus))
        for at, (left, right) in enumerate(rows):
            band[tap, at * 128 : at * 128 + 128, 0:128] = left
            band[tap, at * 128 : at * 128 + 128, 128:256] = right


def assemble(side, halo, nb, sources, cols):
    row = iota((8, LANES + 2 * halo), 0)

    def source(brick, tap):
        number = nb[brick, tap]
        return jnp.where(number < 0, BRICKS, lax.rem(number, BRICKS))

    @pl.loop(0, BRICKS // 2)
    def _(pair):
        for dx, ref in sources:
            index = [
                [[source(2 * pair + b, 9 * dx + 3 * dy + dz) for dz in range(3)] for dy in range(3)]
                for b in range(2)
            ]
            for plane in range(side if dx == 1 else 1):
                at = slice(8 * plane, 8 * plane + 8)
                shifted = [[], [], []]
                for b in range(2):
                    views = []
                    for dy in range(3):
                        before, here, after = index[b][dy]
                        views.append(
                            jnp.concatenate(
                                [
                                    ref[before, at, LANES - halo : LANES],
                                    ref[here, at, :],
                                    ref[after, at, 0:halo],
                                ],
                                axis=1,
                            )
                        )
                    back, mid, front = views
                    shifted[0].append(
                        jnp.where(
                            row == 0,
                            pltpu.roll(back, (9 - side) % 8, 0),
                            pltpu.roll(mid, 1, 0),
                        )
                    )
                    shifted[1].append(mid)
                    shifted[2].append(
                        jnp.where(
                            row == side - 1,
                            pltpu.roll(front, side - 1, 0),
                            pltpu.roll(mid, 7, 0),
                        )
                    )
                to = plane + 1 if dx == 1 else (0 if dx == 0 else side + 1)
                rows = pl.ds(pl.multiple_of(16 * pair, 16), 16)
                for c in range(3):
                    cols[c, to, rows, :] = jnp.concatenate(shifted[c], axis=0).astype(BF16)


def convolve(side, depth, cols, weights, finish):
    chunk = min(side, 4)
    matrix = jnp.concatenate([weights(tap) for tap in range(9)], axis=0)
    for half in range(2):
        lanes = slice(256 * half, 256 * half + depth)
        for first in range(0, side, chunk):
            left = jnp.concatenate(
                [
                    cols[c, first + a : first + a + chunk, :, lanes].reshape(chunk * 64, depth)
                    for a in range(3)
                    for c in range(3)
                ],
                axis=1,
            )
            sums = jnp.dot(left, matrix, preferred_element_type=F32)
            finish(half, first, sums.reshape(chunk, BRICKS, 8, 256))


def rounded(value):
    return value.astype(BF16).astype(F32)


def pool_bits(bits, fine_side, temp, pooled):
    half = fine_side // 2
    count = BRICKS * half * 8
    joined = bits[0 : BRICKS * fine_side * 8, :].reshape(BRICKS * half, 2, 8, 128)
    temp[0:count, :] = (joined[:, 0] | joined[:, 1]).reshape(count, 128)
    temp[count : count + 16, :] = jnp.zeros((16, 128), jnp.int32)
    for at in range(BRICKS * half):
        even = temp[pl.ds(8 * at, 8, stride=2), :]
        odd = temp[pl.ds(8 * at + 1, 8, stride=2), :]
        pooled[8 * at : 8 * at + 8, :] = even | odd


def reduce_level(side, block, fine, kernel, bits, bit_width, emit):
    half = side // 2
    width = 2 * block
    for at in range(LANES // width):
        parts = []
        for ci in range(2):
            for cj in range(2):
                pieces = []
                for lane in range(at * width, (at + 1) * width, 128):
                    pieces.append(
                        jnp.concatenate(
                            [
                                fine[lane // 128, pl.ds((b * side + 2 * i + ci) * 8 + cj, 8, stride=2), :]
                                for b in range(BRICKS)
                                for i in range(half)
                            ],
                            axis=0,
                        )
                    )
                parts += pieces
        left = jnp.concatenate(parts, axis=1).astype(BF16)
        sums = jnp.dot(left, kernel, preferred_element_type=F32)
        mask = ((bits[0 : BRICKS * half * 8, :] >> (bit_width * at)) & ((1 << bit_width) - 1)) != 0
        wide = sums.shape[1]
        for lane in range(0, wide, 128):
            emit(
                at * wide + lane,
                jnp.where(mask, jnp.maximum(sums[:, lane : lane + 128], 0.0), 0.0),
            )


def relayout(temp, lane):
    for q in range(4):
        even = temp[pl.ds(2 * q, 64, stride=8), :]
        odd = temp[pl.ds(2 * q + 1, 64, stride=8), :]
        yield q, jnp.where(lane < 64, even, pltpu.roll(odd, 64, 1))


def fused(nb, feat, occ, conv_one, kernel_one, conv_two_hbm, kernel_two_hbm, conv_three_hbm,
          out_one, out_two, cols_three, bits_three, conv_three,
          own_one, own_two, own_three, low, high, cols_one, cols_two,
          band_one, band_two, conv_two, kernel_two,
          fine, temp, wide, bits_one, bits_two, bits_temp,
          outgoing, incoming, load_sems, send_sems, recv_sems):
    me = lax.axis_index("morton")
    count = lax.axis_size("morton")
    has_low, has_high = me > 0, me < count - 1
    sides = ((has_low, me - 1), (has_high, me + 1))

    loads = [
        pltpu.make_async_copy(source, target, load_sems.at[at])
        for at, (source, target) in enumerate(
            ((conv_two_hbm, conv_two), (kernel_two_hbm, kernel_two), (conv_three_hbm, conv_three))
        )
    ]
    for load in loads:
        load.start()

    barrier = pltpu.get_barrier_semaphore()
    for there, device in sides:
        @pl.when(there)
        def _():
            pl.semaphore_signal(barrier, inc=1, device_id={"morton": device},
                                device_id_type=pl.DeviceIdType.MESH)

    def transfer(level, to):
        return pltpu.make_async_remote_copy(
            src_ref=outgoing.at[level, to],
            dst_ref=incoming.at[level, 1 - to],
            send_sem=send_sems.at[level, to],
            recv_sem=recv_sems.at[level, 1 - to],
            device_id={"morton": sides[to][1]},
            device_id_type=pl.DeviceIdType.MESH,
        )

    def send(level):
        for to in range(2):
            @pl.when(sides[to][0])
            def _():
                transfer(level, to).start()

    def receive(level):
        for source in range(2):
            @pl.when(sides[source][0])
            def _():
                transfer(level, 1 - source).wait_recv()
                (low, high)[source][0:BRICKS] = incoming[level, source].astype(F32)

    lane = iota((64, 128), 1)
    row = iota((64, 16), 0)
    column = iota((64, 16), 1)
    upper = (lane >= 64).astype(jnp.int32)
    for ref in (own_one, own_two, own_three):
        ref[BRICKS] = jnp.zeros(ref.shape[1:], F32)
    for ref in (low, high):
        ref[...] = jnp.zeros(ref.shape, F32)

    @pl.loop(0, BRICKS)
    def _(b):
        words = jnp.broadcast_to(occ[pl.ds(b, 1), :], (64, 16))
        octet = (words >> (8 * (row % 4))) & 255
        picked = jnp.where(column == row // 4, octet.astype(F32), 0.0)
        mask = jnp.broadcast_to(jnp.sum(picked, axis=1, keepdims=True), (64, 128)).astype(jnp.int32)
        bits_one[pl.ds(pl.multiple_of(64 * b, 64), 64), :] = mask
        temp[:, 0:64] = feat[b].astype(F32).T
        for q, both in relayout(temp, lane):
            value = jnp.where(((mask >> (2 * q + upper)) & 1) != 0, both, 0.0)
            lanes = slice(128 * q, 128 * q + 128)
            own_one[b, :, lanes] = value
            outgoing[0, 0, b, :, lanes] = value[0:8].astype(BF16)
            outgoing[0, 1, b, :, lanes] = value[56:64].astype(BF16)

    pl.semaphore_wait(barrier, jnp.minimum(me, 1) + jnp.minimum(count - 1 - me, 1))
    send(0)
    band_pairs(conv_one, band_one)
    assemble(8, 128, nb, ((1, own_one),), cols_one)
    loads[0].wait()
    band_single(conv_two, band_two)
    receive(0)
    assemble(8, 128, nb, ((0, low), (2, high)), cols_one)

    small_upper = (iota((8, 128), 1) >= 64).astype(jnp.int32)

    def finish_one(half, first, sums):
        for p in range(sums.shape[0]):
            for b in range(BRICKS):
                at = b * 64 + (first + p) * 8
                mask = bits_one[at : at + 8, :]
                for part in range(2):
                    q = 2 * half + part
                    fine[q, at : at + 8, :] = rounded(
                        jnp.where(
                            ((mask >> (2 * q + small_upper)) & 1) != 0,
                            jnp.maximum(sums[p, b, :, 128 * part : 128 * part + 128], 0.0),
                            0.0,
                        )
                    )

    convolve(8, 512, cols_one, lambda tap: band_one[tap], finish_one)
    fine[:, 512:528, :] = jnp.zeros((4, 16, 128), F32)
    pool_bits(bits_one, 8, bits_temp, bits_two)

    def emit_into(own, level, planes):
        def emit(lane_at, value):
            value = rounded(value).reshape(BRICKS, 8 * planes, 128)
            lanes = slice(lane_at, lane_at + 128)
            own[0:BRICKS, :, lanes] = value
            outgoing[level, 0, :, :, lanes] = value[:, 0:8].astype(BF16)
            outgoing[level, 1, :, :, lanes] = value[:, 8 * planes - 8 :].astype(BF16)
        return emit

    reduce_level(8, 64, fine, kernel_one[...], bits_two, 2, emit_into(own_two, 1, 4))
    send(1)
    assemble(4, 128, nb, ((1, own_two),), cols_two)

    @pl.loop(0, BRICKS)
    def _(b):
        for q in range(4):
            both = fine[q, pl.ds(pl.multiple_of(64 * b, 64), 64), :]
            wide[pl.ds(2 * q, 64, stride=8), :] = both
            wide[pl.ds(2 * q + 1, 64, stride=8), :] = pltpu.roll(both, 64, 1)
        out_one[b] = wide[:, 0:64].T.astype(BF16)

    receive(1)
    assemble(4, 128, nb, ((0, low), (2, high)), cols_two)

    def finish_two(half, first, sums):
        for p in range(sums.shape[0]):
            for b in range(BRICKS):
                at = b * 32 + (first + p) * 8
                mask = bits_two[at : at + 8, :]
                for part in range(2):
                    q = 2 * half + part
                    fine[q, at : at + 8, :] = rounded(
                        jnp.where(
                            ((mask >> (2 * q)) & 3) != 0,
                            jnp.maximum(sums[p, b, :, 128 * part : 128 * part + 128], 0.0),
                            0.0,
                        )
                    )

    convolve(4, 512, cols_two, lambda tap: band_two[tap], finish_two)
    pool_bits(bits_two, 4, bits_temp, bits_three)
    loads[1].wait()
    reduce_level(4, 128, fine, kernel_two[...], bits_three, 4, emit_into(own_three, 2, 2))
    send(2)
    assemble(2, 256, nb, ((1, own_three),), cols_three)
    for b in range(BRICKS):
        for i in range(4):
            for k in range(4):
                at = b * 32 + 8 * i
                wide[pl.ds(64 * b + 16 * i + k, 4, stride=4), :] = fine[k, at : at + 4, :]
    out_two[...] = wide[...].reshape(BRICKS, 64, 128).astype(BF16)
    receive(2)
    assemble(2, 256, nb, ((0, low), (2, high)), cols_three)

    loads[2].wait()
    for level in range(3):
        for to in range(2):
            @pl.when(sides[to][0])
            def _():
                transfer(level, to).wait_send()


def last_level(one, two, cols_three, bits_three, conv_three,
               out_one, out_two, out_three, wide_three):
    out_one[...] = one[...]
    out_two[...] = two[...]

    def finish_three(half, first, sums):
        for p in range(sums.shape[0]):
            for b in range(BRICKS):
                at = b * 16 + (first + p) * 8
                mask = ((bits_three[at : at + 8, :] >> (4 * half)) & 15) != 0
                for part in range(2):
                    value = jnp.where(
                        mask, jnp.maximum(sums[p, b, :, 128 * part : 128 * part + 128], 0.0), 0.0
                    )
                    wide_three[part, pl.ds(8 * b + 4 * (first + p) + half, 2, stride=2), :] = value[0:2]

    convolve(2, 768, cols_three, lambda tap: conv_three[3 * tap : 3 * tap + 3].reshape(768, 256), finish_three)
    for part in range(2):
        out_three[:, :, 128 * part : 128 * part + 128] = (
            wide_three[part].reshape(BRICKS, 8, 128).astype(BF16)
        )


def on_device(features, neighbours, occupancy, conv_one, first_reduce_kernel,
              conv_two, second_reduce_kernel, conv_three):
    vm = pl.BlockSpec(memory_space=pltpu.VMEM)
    hbm = pl.BlockSpec(memory_space=pltpu.HBM)
    kernel_two = second_reduce_kernel.reshape(1024, 256)
    scratch = [
        ((BRICKS + 1, 64, LANES), F32), ((BRICKS + 1, 32, LANES), F32),
        ((BRICKS + 1, 16, LANES), F32), ((BRICKS + 1, 8, LANES), F32),
        ((BRICKS + 1, 8, LANES), F32),
        ((3, 10, 64, 768), BF16), ((3, 6, 64, 768), BF16),
        ((9, 512, 256), BF16), ((9, 512, 256), BF16),
        (conv_two.shape, BF16), (kernel_two.shape, BF16),
        ((4, 528, 128), F32), ((512, 128), F32), ((512, 128), F32),
        ((512, 128), jnp.int32), ((256, 128), jnp.int32),
        ((272, 128), jnp.int32),
        ((3, 2, BRICKS, 8, LANES), BF16), ((3, 2, BRICKS, 8, LANES), BF16),
    ]
    shapes = [
        jax.ShapeDtypeStruct((BRICKS, 64, 512), BF16),
        jax.ShapeDtypeStruct((BRICKS, 64, 128), BF16),
    ]
    first, second, cols, bits, weights = pl.pallas_call(
        fused,
        out_shape=shapes
        + [
            jax.ShapeDtypeStruct((3, 4, 64, 1024), BF16),
            jax.ShapeDtypeStruct((128, 128), jnp.int32),
            jax.ShapeDtypeStruct(conv_three.shape, BF16),
        ],
        in_specs=[pl.BlockSpec(memory_space=pltpu.SMEM), vm, vm, vm, vm, hbm, hbm, hbm],
        out_specs=[vm] * 5,
        scratch_shapes=[pltpu.VMEM(shape, dtype) for shape, dtype in scratch]
        + [pltpu.SemaphoreType.DMA((3,)), pltpu.SemaphoreType.DMA((3, 2)),
           pltpu.SemaphoreType.DMA((3, 2))],
        compiler_params=pltpu.CompilerParams(
            collective_id=0, has_side_effects=True, vmem_limit_bytes=36 << 20
        ),
    )(*(
        pltpu.with_memory_space_constraint(x, pltpu.HBM)
        for x in (neighbours, jnp.swapaxes(features, 1, 2), occupancy, conv_one,
                  first_reduce_kernel.reshape(512, 128), conv_two, kernel_two, conv_three)
    ))
    first, second, third = pl.pallas_call(
        last_level,
        out_shape=shapes + [jax.ShapeDtypeStruct((BRICKS, 8, 256), BF16)],
        in_specs=[vm] * 5,
        out_specs=[vm] * 3,
        scratch_shapes=[pltpu.VMEM((2, 64, 128), F32)],
        compiler_params=pltpu.CompilerParams(vmem_limit_bytes=16 << 20),
    )(first, second, cols, bits, weights)
    return jnp.swapaxes(first, 1, 2), second, third


def solution(mesh):
    split = P(("tiles", "morton"), None, None)
    flat = P(("tiles", "morton"), None)
    return jax.shard_map(
        on_device,
        mesh=mesh,
        in_specs=(split, flat, flat, P(), P(), P(), P(), P()),
        out_specs=(split, split, split),
        check_vma=False,
    )
```
